512 devices in a mesh: src: 32 (over y_hi, x, core), tgt: 16 (over z, y_lo).
Axes of the slice: x: 4, y: 8 (y_hi: 4, y_lo: 2; y = y_hi * 2 + y_lo), z: 8, core: 2. Of those that a mesh axis runs over, the one named last changes fastest.
Arguments:
- feat_in: bfloat16 [512, 49, 128], P(('src', 'tgt')), may hold values from -6 to 6
- ffn_in: bfloat16 [512, 49, 128], P(('src', 'tgt')), may hold values from -6 to 6
- grad_out: bfloat16 [512, 49, 128], P(('src', 'tgt')), may hold values from -6 to 6
- ffn_up: bfloat16 [128, 512], replicated, may hold values from -0.5 to 0.5
- ffn_down: bfloat16 [512, 128], replicated, may hold values from -0.25 to 0.25
- so2_zero: bfloat16 [896, 1024], P('tgt'), may hold values from -0.1875 to 0.1875
- so2_one: bfloat16 [2, 768, 768], P(None, 'tgt'), may hold values from -0.15625 to 0.15625
- so2_two: bfloat16 [2, 640, 640], P(None, 'tgt'), may hold values from -0.15625 to 0.15625
- wigner: bfloat16 [64, 29, 49], replicated, may hold values from -1 to 1
- edge_src: int32 [32, 16, 128], P('src', 'tgt'), may hold values from 0 to 15
- edge_tgt: int32 [32, 16, 128], P('src', 'tgt'), may hold values from 0 to 31
- edge_angle: int32 [32, 16, 128], P('src', 'tgt'), may hold values from 0 to 63
- edge_radial: bfloat16 [32, 16, 128, 128], P('src', 'tgt'), may hold values from 0.25 to 2
- edge_count: int32 [32, 16], P('src', 'tgt'), may hold values from 1 to 128, as said below
Outputs:
- feat_grad: bfloat16 [512, 49, 128], P(('src', 'tgt'))
The draws below stay inside these ranges and needn't reach their ends.
Inputs may be any that keep to these rules, and one draw needn't show every extreme that they name: The slots of a block at or past its edge_count are padding. Some block holds 128 edges.
All inputs are finite; a program needn't handle non-finite values.
Results may differ from the reference program's by a relative error of at most 0.006.
Values may be sent and summed in bfloat16 or wider, within the bound.
No kernel may reach another device: no remote copies, remote signals or barrier semaphores. Data moves between devices by JAX's collectives and lax.ppermute only.
A program may use at most 64 MiB of HBM per device.

```python
import math
import jax
import jax.numpy as jnp
import numpy as np
from jax import lax

C = 128
HID = 512
LMAX = 6
GRID_SIDE = 14
N_ANG = 64
ATOM_DEV = 1
E_CAP = 128
COEF = 49
KEEP = 29
SRC_GRP = 16
TGT_GRP = 32
ATOMS = 512
N_SRC = 32
N_TGT = 16


def draw_wigner(key, part):
    rotations = jnp.zeros((N_ANG, KEEP, COEF), jnp.float32)
    blocks = []
    for degree in range(LMAX + 1):
        width_here = 2 * degree + 1
        gaussian = jax.random.normal(jax.random.fold_in(key, 11 + degree), (N_ANG, width_here, width_here), jnp.float32)
        blocks.append(jnp.linalg.qr(gaussian)[0])
    row_index = 0
    for order_m in [0, 1, -1, 2, -2]:
        for degree in range(abs(order_m), LMAX + 1):
            rotations = rotations.at[:, row_index, degree * degree:(degree + 1) * (degree + 1)].set(blocks[degree][:, degree + order_m, :])
            row_index = row_index + 1
    return rotations.astype(jnp.bfloat16)


def draw_edge_count(key, part):
    levels = jax.random.randint(jax.random.fold_in(key, 31), (N_SRC * N_TGT,), 0, 16)
    chosen = jax.random.randint(jax.random.fold_in(key, 32), (), 0, N_SRC * N_TGT)
    levels = jnp.where(jnp.arange(N_SRC * N_TGT) == chosen, 15, levels)
    counts = 1 + (E_CAP - 1) * (levels + 1) * (levels + 1) // 256
    return counts.reshape(N_SRC, N_TGT).astype(jnp.int32)


def with_ends(drawn, own_key, smallest, top_value):
    index_at = [jax.random.randint(jax.random.fold_in(own_key, axis), (), 0, length) for axis, length in enumerate(drawn.shape)]
    longest = drawn.shape.index(max(drawn.shape))
    neighbour = index_at[:longest] + [(index_at[longest] + 1) % drawn.shape[longest]] + index_at[longest + 1:]
    return drawn.at[tuple(index_at)].set(smallest).at[tuple(neighbour)].set(top_value)


def level_of(stream_key, shape, split, smallest, high):
    def one(position, blocks):
        steps = jax.random.uniform(jax.random.fold_in(jax.random.fold_in(stream_key, 6), position), (blocks,), jnp.float32, smallest / len(split), high / len(split))
        return jnp.repeat(jnp.exp(steps), shape[position] // blocks).reshape((-1,) + (1,) * (len(shape) - position - 1))

    factor_of = one(*split[0])
    for cut in split[1:]:
        factor_of = factor_of * one(*cut)
    return factor_of


def bell_draw(key, extent, deviation, bound, pieces=(), held_as=jnp.bfloat16):
    array = deviation * jax.random.normal(key, extent, jnp.float32)
    if pieces:
        array = array * level_of(key, extent, pieces, -0.22, 0.18)
    return jnp.clip(array, -bound, bound).astype(held_as)


def setup_inputs(seed: int = 0) -> dict:
    seeds = jax.random.split(jax.random.key(seed), 15)
    return {
        "feat_in": bell_draw(seeds[0], (ATOMS, COEF, C), 1.0, 6.0, ((0, 512),)),
        "ffn_in": bell_draw(seeds[1], (ATOMS, COEF, C), 1.0, 6.0, ((0, 512),)),
        "grad_out": bell_draw(seeds[2], (ATOMS, COEF, C), 1.0, 6.0, ((0, 512),)),
        "ffn_up": bell_draw(seeds[3], (C, HID), C ** -0.5, 0.5),
        "ffn_down": bell_draw(seeds[4], (HID, C), HID ** -0.5, 0.25),
        "so2_zero": bell_draw(seeds[5], ((LMAX + 1) * C, (LMAX + 2) * C), ((LMAX + 1) * C) ** -0.5, 0.1875, ((0, 16),)),
        "so2_one": bell_draw(seeds[6], (2, LMAX * C, LMAX * C), (2 * LMAX * C) ** -0.5, 0.15625, ((1, 16),)),
        "so2_two": bell_draw(seeds[7], (2, (LMAX - 1) * C, (LMAX - 1) * C), (2 * (LMAX - 1) * C) ** -0.5, 0.15625, ((1, 16),)),
        "wigner": draw_wigner(jax.random.fold_in(seeds[14], 71), 0),
        "edge_src": with_ends(jax.random.randint(seeds[9], (N_SRC, N_TGT, E_CAP), 0, SRC_GRP), jax.random.fold_in(seeds[9], 1), 0, SRC_GRP - 1).astype(jnp.int32),
        "edge_tgt": with_ends(jax.random.randint(seeds[10], (N_SRC, N_TGT, E_CAP), 0, TGT_GRP), jax.random.fold_in(seeds[10], 1), 0, TGT_GRP - 1).astype(jnp.int32),
        "edge_angle": with_ends(jax.random.randint(seeds[11], (N_SRC, N_TGT, E_CAP), 0, N_ANG), jax.random.fold_in(seeds[11], 1), 0, N_ANG - 1).astype(jnp.int32),
        "edge_radial": jnp.clip(jnp.exp(math.log(2.0) - 2.0794415 * jax.random.uniform(seeds[12], (N_SRC, N_TGT, E_CAP, C), jnp.float32) ** level_of(seeds[12], (N_SRC, N_TGT, E_CAP, C), ((0, 32), (1, 16)), -0.2, 0.2)), 0.25, 2.0).astype(jnp.bfloat16),
        "edge_count": draw_edge_count(jax.random.fold_in(seeds[14], 71), 0),
    }


message_scale = 0.125

def sphere_tables(degree_max, grid_side):
    polar_angle = (np.arange(grid_side) + 0.5) * np.pi / grid_side
    azimuth = np.arange(grid_side) * 2.0 * np.pi / grid_side
    cosine = np.cos(polar_angle)
    sine_theta = np.sin(polar_angle)
    coef_count = (degree_max + 1) * (degree_max + 1)
    harmonics = np.zeros((grid_side, grid_side, coef_count))
    for order_m in range(degree_max + 1):
        diagonal = np.ones(grid_side)
        for factor in range(1, order_m + 1):
            diagonal = diagonal * (2 * factor - 1) * sine_theta
        legendre = {order_m: diagonal}
        if order_m + 1 <= degree_max:
            legendre[order_m + 1] = cosine * (2 * order_m + 1) * diagonal
        for degree in range(order_m + 2, degree_max + 1):
            legendre[degree] = ((2 * degree - 1) * cosine * legendre[degree - 1] - (degree + order_m - 1) * legendre[degree - 2]) / (degree - order_m)
        for degree in range(order_m, degree_max + 1):
            scaling = math.sqrt((2 * degree + 1) / (4.0 * math.pi) * math.factorial(degree - order_m) / math.factorial(degree + order_m))
            if order_m > 0:
                scaling = scaling * math.sqrt(2.0)
            polar_part = scaling * legendre[degree]
            centre = degree * degree + degree
            harmonics[:, :, centre + order_m] = polar_part[:, None] * np.cos(order_m * azimuth)[None, :]
            if order_m > 0:
                harmonics[:, :, centre - order_m] = polar_part[:, None] * np.sin(order_m * azimuth)[None, :]
    to_grid = harmonics.reshape(grid_side * grid_side, coef_count)
    quadrature = np.repeat(sine_theta * (np.pi / grid_side) * (2.0 * np.pi / grid_side), grid_side)
    from_grid = (to_grid * quadrature[:, None]).T
    return (jnp.asarray(to_grid, jnp.float32).astype(jnp.bfloat16), jnp.asarray(from_grid, jnp.float32).astype(jnp.bfloat16))

def ffn_backward(ffn_rows, grad_rows, ffn_up, ffn_down, to_grid, from_grid):
    atom_count, coef_count, channels = ffn_rows.shape
    grid_feat = jnp.einsum('pk,akc->apc', to_grid.astype(jnp.float32), ffn_rows.astype(jnp.float32)).astype(jnp.bfloat16)
    grid_points = grid_feat.shape[1]
    pre_act = jnp.dot(grid_feat.reshape(atom_count * grid_points, channels).astype(jnp.float32), ffn_up.astype(jnp.float32), preferred_element_type=jnp.float32)
    grad_value = jnp.einsum('kp,akc->apc', from_grid.astype(jnp.float32), grad_rows.astype(jnp.float32)).astype(jnp.bfloat16)
    grad_act = jnp.dot(grad_value.reshape(atom_count * grid_points, channels).astype(jnp.float32), ffn_down.T.astype(jnp.float32), preferred_element_type=jnp.float32)
    sigmoid_pre = jax.nn.sigmoid(pre_act)
    grad_pre = (grad_act * sigmoid_pre * (1.0 + pre_act * (1.0 - sigmoid_pre))).astype(jnp.bfloat16)
    grad_grid = jnp.dot(grad_pre.astype(jnp.float32), ffn_up.T.astype(jnp.float32), preferred_element_type=jnp.float32).astype(jnp.bfloat16)
    ffn_term = jnp.einsum('pk,apc->akc', to_grid.astype(jnp.float32), grad_grid.reshape(atom_count, grid_points, channels).astype(jnp.float32))
    return (grad_rows.astype(jnp.float32) + ffn_term).astype(jnp.bfloat16)

def matmul_plain(left, right):
    return jnp.dot(left.astype(jnp.float32), right.astype(jnp.float32), preferred_element_type=jnp.float32)

def matmul_flip(left, right):
    return jnp.dot(left.astype(jnp.float32), right.T.astype(jnp.float32), preferred_element_type=jnp.float32)

def so2_forward(rotated, w_zero, w_one, w_two, degree_max, channels):
    cut_a = (degree_max + 1) * channels
    cut_b = cut_a + degree_max * channels
    cut_c = cut_b + degree_max * channels
    cut_d = cut_c + (degree_max - 1) * channels
    zero_part = rotated[:, :cut_a]
    one_plus = rotated[:, cut_a:cut_b]
    one_minus = rotated[:, cut_b:cut_c]
    two_plus = rotated[:, cut_c:cut_d]
    two_minus = rotated[:, cut_d:]
    out_zero = matmul_plain(zero_part, w_zero)
    out_one_plus = matmul_plain(one_plus, w_one[0]) - matmul_plain(one_minus, w_one[1])
    out_one_minus = matmul_plain(one_minus, w_one[0]) + matmul_plain(one_plus, w_one[1])
    out_two_plus = matmul_plain(two_plus, w_two[0]) - matmul_plain(two_minus, w_two[1])
    out_two_minus = matmul_plain(two_minus, w_two[0]) + matmul_plain(two_plus, w_two[1])
    return jnp.concatenate([out_zero, out_one_plus, out_one_minus, out_two_plus, out_two_minus], axis=1)

def so2_backward(grad_pre, w_zero, w_one, w_two, degree_max, channels):
    cut_a = (degree_max + 2) * channels
    cut_b = cut_a + degree_max * channels
    cut_c = cut_b + degree_max * channels
    cut_d = cut_c + (degree_max - 1) * channels
    grad_zero = grad_pre[:, :cut_a]
    grad_one_plus = grad_pre[:, cut_a:cut_b]
    grad_one_minus = grad_pre[:, cut_b:cut_c]
    grad_two_plus = grad_pre[:, cut_c:cut_d]
    grad_two_minus = grad_pre[:, cut_d:]
    back_zero = matmul_flip(grad_zero, w_zero)
    back_one_plus = matmul_flip(grad_one_plus, w_one[0]) + matmul_flip(grad_one_minus, w_one[1])
    back_one_minus = matmul_flip(grad_one_minus, w_one[0]) - matmul_flip(grad_one_plus, w_one[1])
    back_two_plus = matmul_flip(grad_two_plus, w_two[0]) + matmul_flip(grad_two_minus, w_two[1])
    back_two_minus = matmul_flip(grad_two_minus, w_two[0]) - matmul_flip(grad_two_plus, w_two[1])
    return jnp.concatenate([back_zero, back_one_plus, back_one_minus, back_two_plus, back_two_minus], axis=1)

def gate_backward(hidden, grad_o, degree_max):
    gate_index = degree_max + 1
    scalar_pre = hidden[:, 0]
    gate_pre = hidden[:, gate_index]
    sigmoid_gate = jax.nn.sigmoid(gate_pre)
    sigmoid_scalar = jax.nn.sigmoid(scalar_pre)
    grad_scalar = grad_o[:, 0] * sigmoid_scalar * (1.0 + scalar_pre * (1.0 - sigmoid_scalar))
    gated_rows = jnp.concatenate([hidden[:, 1:gate_index], hidden[:, gate_index + 1:]], axis=1)
    grad_rows = grad_o[:, 1:]
    grad_gate = lax.optimization_barrier(jnp.sum(grad_rows * gated_rows, axis=1)) * sigmoid_gate * (1.0 - sigmoid_gate)
    grad_gated = grad_rows * sigmoid_gate[:, None, :]
    return jnp.concatenate([grad_scalar[:, None], grad_gated[:, :degree_max], grad_gate[:, None], grad_gated[:, degree_max:]], axis=1)

def block_grad(source_group, target_group, src_ids, tgt_ids, angle_ids, radial, live_count, so2_zero, so2_one, so2_two, wigner):
    slot_count = src_ids.shape[0]
    rotation = wigner[angle_ids].astype(jnp.float32)
    source_rows = source_group[src_ids].astype(jnp.float32)
    rotated = jnp.einsum('erk,ekc->erc', rotation, source_rows).astype(jnp.bfloat16)
    hidden = so2_forward(rotated.reshape(slot_count, KEEP * C), so2_zero, so2_one, so2_two, LMAX, C)
    radial_gain = radial.astype(jnp.float32)[:, None, :]
    hidden = hidden.reshape(slot_count, KEEP + 1, C) * radial_gain
    target_rows = target_group[tgt_ids].astype(jnp.float32)
    grad_o = jnp.einsum('erk,ekc->erc', rotation, target_rows) * message_scale
    grad_hidden = gate_backward(hidden, grad_o, LMAX)
    grad_pre = (grad_hidden * radial_gain).astype(jnp.bfloat16).reshape(slot_count, (KEEP + 1) * C)
    grad_rot = so2_backward(grad_pre, so2_zero, so2_one, so2_two, LMAX, C).astype(jnp.bfloat16).reshape(slot_count, KEEP, C)
    grad_edge = jnp.einsum('erk,erc->ekc', rotation, grad_rot.astype(jnp.float32)).astype(jnp.bfloat16)
    live_slot = jnp.arange(slot_count, dtype=jnp.int32) < live_count
    masked = jnp.where(live_slot[:, None, None], grad_edge.astype(jnp.float32), jnp.zeros((), jnp.float32))
    return jax.ops.segment_sum(masked, src_ids, num_segments=SRC_GRP)

def reference(feat_in, ffn_in, grad_out, ffn_up, ffn_down, so2_zero, so2_one, so2_two, wigner, edge_src, edge_tgt, edge_angle, edge_radial, edge_count):
    to_grid, from_grid = sphere_tables(LMAX, GRID_SIDE)

    def ffn_group(group_items):
        return ffn_backward(group_items[0], group_items[1], ffn_up, ffn_down, to_grid, from_grid)
    target_grad = lax.map(ffn_group, (ffn_in.reshape(N_SRC, SRC_GRP, COEF, C), grad_out.reshape(N_SRC, SRC_GRP, COEF, C)))
    target_grad = target_grad.reshape(ATOMS, COEF, C)
    source_groups = feat_in.reshape(N_SRC, SRC_GRP, COEF, C)
    target_groups = target_grad.reshape(N_SRC, N_TGT, ATOM_DEV, COEF, C).transpose(1, 0, 2, 3, 4).reshape(N_TGT, TGT_GRP, COEF, C)

    def per_source(group_items):
        source_group, src_row, tgt_row, angle_row, radial_row, count_row = group_items

        def per_target(running, block_items):
            target_group, src_ids, tgt_ids, angle_ids, radial, live_count = block_items
            return (running + block_grad(source_group, target_group, src_ids, tgt_ids, angle_ids, radial, live_count, so2_zero, so2_one, so2_two, wigner), None)
        running, unused = lax.scan(per_target, jnp.zeros((SRC_GRP, COEF, C), jnp.float32), (target_groups, src_row, tgt_row, angle_row, radial_row, count_row))
        return running
    summed = lax.map(per_source, (source_groups, edge_src, edge_tgt, edge_angle, edge_radial, edge_count))
    return (target_grad.astype(jnp.float32) + summed.reshape(ATOMS, COEF, C)).astype(jnp.bfloat16)
```

```python
import math

import jax
import jax.numpy as jnp
import numpy as np
from jax import lax
from jax.experimental import pallas as pl
from jax.experimental.pallas import tpu as pltpu
from jax.sharding import Mesh
from jax.sharding import PartitionSpec as P

LMAX = 6
GRID_SIDE = 14
C = 128
KEEP = 29
COEF = 49
PAD = 56
message_scale = 0.125
BF = jnp.bfloat16
F32 = jnp.float32
VMEM = pltpu.VMEM
ROWS = 768
PAIR_ZERO, PAIR_ONE, PAIR_TWO = 0, 448, 1024
PAIR_FEAT, PAIR_ROWS = 1424, 1536


def sphere_tables(degree_max, grid_side):
    polar_angle = (np.arange(grid_side) + 0.5) * np.pi / grid_side
    azimuth = np.arange(grid_side) * 2.0 * np.pi / grid_side
    cosine = np.cos(polar_angle)
    sine_theta = np.sin(polar_angle)
    coef_count = (degree_max + 1) * (degree_max + 1)
    harmonics = np.zeros((grid_side, grid_side, coef_count))
    for order_m in range(degree_max + 1):
        diagonal = np.ones(grid_side)
        for factor in range(1, order_m + 1):
            diagonal = diagonal * (2 * factor - 1) * sine_theta
        legendre = {order_m: diagonal}
        if order_m + 1 <= degree_max:
            legendre[order_m + 1] = cosine * (2 * order_m + 1) * diagonal
        for degree in range(order_m + 2, degree_max + 1):
            legendre[degree] = (
                (2 * degree - 1) * cosine * legendre[degree - 1]
                - (degree + order_m - 1) * legendre[degree - 2]
            ) / (degree - order_m)
        for degree in range(order_m, degree_max + 1):
            scaling = math.sqrt(
                (2 * degree + 1)
                / (4.0 * math.pi)
                * math.factorial(degree - order_m)
                / math.factorial(degree + order_m)
            )
            if order_m > 0:
                scaling = scaling * math.sqrt(2.0)
            polar_part = scaling * legendre[degree]
            centre = degree * degree + degree
            harmonics[:, :, centre + order_m] = (
                polar_part[:, None] * np.cos(order_m * azimuth)[None, :]
            )
            if order_m > 0:
                harmonics[:, :, centre - order_m] = (
                    polar_part[:, None] * np.sin(order_m * azimuth)[None, :]
                )
    to_grid = harmonics.reshape(grid_side * grid_side, coef_count)
    quadrature = np.repeat(sine_theta * (np.pi / grid_side) * (2.0 * np.pi / grid_side), grid_side)
    from_grid = (to_grid * quadrature[:, None]).T
    return to_grid.astype(np.float32), from_grid.astype(np.float32)


def dot(left, right):
    return jnp.dot(left, right, preferred_element_type=F32)


def dot_nt(left, right):
    return lax.dot_general(left, right, (((1,), (1,)), ((), ())), preferred_element_type=F32)


def pack_kernel(place, zero_ref, one_ref, two_ref, feat_ref, out_ref):
    for side in range(2):

        @pl.when(place[0] == side)
        def _():
            for block in range(4):
                column = 512 * side + 128 * block
                out_ref[56 * block : 56 * block + 56, :] = zero_ref[:, column : column + 128]
            for block in range(6):
                out_ref[224 + 48 * block : 272 + 48 * block, :] = one_ref[
                    side, :, 128 * block : 128 * block + 128
                ]
            for block in range(5):
                out_ref[512 + 40 * block : 552 + 40 * block, :] = two_ref[
                    side, :, 128 * block : 128 * block + 128
                ]

    out_ref[712:761, :] = feat_ref[0]
    out_ref[761:768, :] = jnp.zeros((7, C), BF)


def pack_own(place, so2_zero, so2_one, so2_two, feat_in):
    return pl.pallas_call(
        pack_kernel,
        out_shape=jax.ShapeDtypeStruct((ROWS, C), BF),
        in_specs=[pl.BlockSpec(memory_space=pltpu.SMEM)] + [pl.BlockSpec(memory_space=VMEM)] * 4,
        out_specs=pl.BlockSpec(memory_space=VMEM),
    )(place, so2_zero, so2_one, so2_two, feat_in)


def pair_kernel(place, own_ref, other_ref, out_ref):
    for side in range(2):

        @pl.when(place[1] == side)
        def _():
            for part, ref in ((side, own_ref), (1 - side, other_ref)):
                for base, pair_base, count, rows in (
                    (0, PAIR_ZERO, 4, 56),
                    (224, PAIR_ONE, 6, 48),
                    (512, PAIR_TWO, 5, 40),
                    (712, PAIR_FEAT, 1, 56),
                ):
                    for block in range(count):
                        start = pair_base + 2 * rows * block + rows * part
                        out_ref[start : start + rows, :] = ref[
                            base + rows * block : base + rows * block + rows, :
                        ]


def pair_up(place, own, other):
    return pl.pallas_call(
        pair_kernel,
        out_shape=jax.ShapeDtypeStruct((PAIR_ROWS, C), BF),
        in_specs=[pl.BlockSpec(memory_space=pltpu.SMEM)] + [pl.BlockSpec(memory_space=VMEM)] * 2,
        out_specs=pl.BlockSpec(memory_space=VMEM),
    )(place, own, other)


def ffn_kernel(x_ref, g_ref, up_ref, down_ref, to_ref, from_ref, back_ref, out_ref, xs, gs):
    xs[0:COEF, :] = x_ref[0]
    xs[COEF:PAD, :] = jnp.zeros((PAD - COEF, C), BF)
    gs[0:COEF, :] = g_ref[0]
    gs[COEF:PAD, :] = jnp.zeros((PAD - COEF, C), BF)
    grid_feat = dot(to_ref[...], xs[...]).astype(BF)
    grad_value = dot(from_ref[...], gs[...]).astype(BF)
    pre_act = dot(grid_feat, up_ref[...])
    grad_act = dot_nt(grad_value, down_ref[...])
    gate = jax.nn.sigmoid(pre_act)
    grad_pre = (grad_act * gate * (1.0 + pre_act * (1.0 - gate))).astype(BF)
    grad_grid = dot_nt(grad_pre, up_ref[...]).astype(BF)
    out_ref[...] = (gs[...].astype(F32) + dot(back_ref[...], grad_grid)).astype(BF)


def ffn_backward(ffn_in, grad_out, ffn_up, ffn_down):
    to_grid, from_grid = sphere_tables(LMAX, GRID_SIDE)
    points = to_grid.shape[0]
    to_pad = np.zeros((208, PAD), np.float32)
    to_pad[:points, :COEF] = to_grid
    from_pad = np.zeros((208, PAD), np.float32)
    from_pad[:points, :COEF] = from_grid.T
    back_pad = np.ascontiguousarray(to_pad.T)
    tables = [jnp.asarray(table, F32).astype(BF) for table in (to_pad, from_pad, back_pad)]
    return pl.pallas_call(
        ffn_kernel,
        out_shape=jax.ShapeDtypeStruct((PAD, C), BF),
        in_specs=[pl.BlockSpec(memory_space=VMEM)] * 7,
        out_specs=pl.BlockSpec(memory_space=VMEM),
        scratch_shapes=[VMEM((PAD, C), BF), VMEM((PAD, C), BF)],
    )(ffn_in, grad_out, ffn_up, ffn_down, *tables)


def rotate_kernel(src, tgt, ang, feat_ref, grad_ref, wig_ref, rot_ref, go_ref, acc):
    slots = 128

    def body(step, carry):
        for lane in range(8):
            slot = step * 8 + lane
            rows = jnp.concatenate([feat_ref[src[slot]], grad_ref[tgt[slot]]], axis=1)
            turned = dot(wig_ref[ang[slot]], rows)
            acc[pl.ds(slot, 32, stride=slots), :] = turned[:, :C]
            go_ref[pl.ds(slot, 32, stride=slots), :] = turned[:, C:]
        return carry

    lax.fori_loop(0, slots // 8, body, 0)
    rot_ref[...] = acc[...].astype(BF)


def rotate_slots(src, tgt, ang, feat, grads, wig):
    smem = pl.BlockSpec(memory_space=pltpu.SMEM)
    vmem = pl.BlockSpec(memory_space=VMEM)
    return pl.pallas_call(
        rotate_kernel,
        out_shape=(
            jax.ShapeDtypeStruct((32 * 128, C), BF),
            jax.ShapeDtypeStruct((32 * 128, C), F32),
        ),
        in_specs=[smem] * 3 + [vmem] * 3,
        out_specs=(vmem, vmem),
        scratch_shapes=[VMEM((32 * 128, C), F32)],
    )(src, tgt, ang, feat, grads, wig)


def edge_kernel(
    place, src, ang, own_ref, other_ref, rot_ref, go_ref, radial_ref, wig_ref, out_ref,
    w_zero, w_one, w_two, hidden, grad_rot, acc,
):
    core = place[0]
    z_here = place[2]
    for half, ref in ((0, own_ref), (1, other_ref)):
        for side in range(2):

            @pl.when((core + half) % 2 == side)
            def _(ref=ref, side=side):
                def piece_body(piece, carry):
                    z_from = lax.rem(z_here + piece, 8)
                    row = pl.ds(pl.multiple_of(z_from * 112, 16), 112)
                    for block in range(4):
                        column = 512 * side + 128 * block
                        w_zero[row, column : column + 128] = ref[
                            piece, PAIR_ZERO + 112 * block : PAIR_ZERO + 112 * block + 112, :
                        ]
                    row = pl.ds(pl.multiple_of(768 * side + z_from * 96, 16), 96)
                    for block in range(6):
                        w_one[row, 128 * block : 128 * block + 128] = ref[
                            piece, PAIR_ONE + 96 * block : PAIR_ONE + 96 * block + 96, :
                        ]
                    row = pl.ds(pl.multiple_of(640 * side + z_from * 80, 16), 80)
                    for block in range(5):
                        w_two[row, 128 * block : 128 * block + 128] = ref[
                            piece, PAIR_TWO + 80 * block : PAIR_TWO + 80 * block + 80, :
                        ]
                    return carry

                lax.fori_loop(0, 8, piece_body, 0)

    def turned(first, count):
        return jnp.concatenate(
            [rot_ref[128 * row : 128 * row + 128, :] for row in range(first, first + count)], axis=1
        )

    radial = radial_ref[...].astype(F32)

    def put(first, rows, value):
        for row in range(rows):
            hidden[128 * (first + row) : 128 * (first + row) + 128, :] = (
                value[:, 128 * row : 128 * row + 128] * radial
            )

    left = turned(0, 7)
    for pair in range(4):
        put(2 * pair, 2, dot(left, w_zero[:, 256 * pair : 256 * pair + 256]))

    def higher(first, count, weight, hidden_first):
        plus = turned(first, count)
        minus = turned(first + count, count)
        both = jnp.concatenate(
            [jnp.concatenate([plus, -minus], axis=1), jnp.concatenate([minus, plus], axis=1)], axis=0
        )
        start = 0
        while start < count:
            wide = min(2, count - start)
            value = dot(both, weight[:, 128 * start : 128 * (start + wide)])
            put(hidden_first + start, wide, value[:128])
            put(hidden_first + count + start, wide, value[128:])
            start = start + wide

    higher(7, 6, w_one, 8)
    higher(19, 5, w_two, 20)

    def hid(row):
        return hidden[128 * row : 128 * row + 128, :]

    def go(row):
        return go_ref[128 * row : 128 * row + 128, :] * message_scale

    scalar_pre = hid(0)
    sigmoid_scalar = jax.nn.sigmoid(scalar_pre)
    sigmoid_gate = jax.nn.sigmoid(hid(7))
    weight_gate = sigmoid_gate * radial
    grads = {}
    grads[0] = (
        go(0) * sigmoid_scalar * (1.0 + scalar_pre * (1.0 - sigmoid_scalar)) * radial
    ).astype(BF)
    total = jnp.zeros((128, C), F32)
    for kept in range(1, KEEP):
        row = kept if kept < 7 else kept + 1
        value = go(kept)
        total = total + value * hid(row)
        grads[row] = (value * weight_gate).astype(BF)
    grads[7] = (total * sigmoid_gate * (1.0 - sigmoid_gate) * radial).astype(BF)

    def side_by_side(first, count):
        return jnp.concatenate([grads[row] for row in range(first, first + count)], axis=1)

    def keep(first, value):
        for row in range(value.shape[1] // 128):
            grad_rot[128 * (first + row) : 128 * (first + row) + 128, :] = value[
                :, 128 * row : 128 * row + 128
            ]

    right = side_by_side(0, 8)
    for start in (0, 2, 4, 6):
        wide = min(2, 7 - start)
        keep(start, dot_nt(right, w_zero[128 * start : 128 * (start + wide), :]))

    def back(first, count, weight, hidden_first):
        both = jnp.concatenate(
            [side_by_side(hidden_first, count), side_by_side(hidden_first + count, count)], axis=0
        )
        start = 0
        span = 128 * count
        while start < count:
            wide = min(2, count - start)
            real = dot_nt(both, weight[128 * start : 128 * (start + wide), :])
            imag = dot_nt(both, weight[span + 128 * start : span + 128 * (start + wide), :])
            keep(first + start, real[:128] + imag[128:])
            keep(first + count + start, real[128:] - imag[:128])
            start = start + wide

    back(7, 6, w_one, 8)
    back(19, 5, w_two, 20)
    grad_rot[KEEP * 128 :, :] = jnp.zeros((3 * 128, C), F32)

    acc[...] = jnp.zeros_like(acc)
    live = place[3]

    def slot_body(step, carry):
        for lane in range(8):
            slot = step * 8 + lane
            rows = grad_rot[pl.ds(slot, 32, stride=128), :]
            rows = jnp.where(slot < live, rows, 0.0).astype(BF)
            acc[src[slot]] += dot(wig_ref[ang[slot]], rows)
        return carry

    lax.fori_loop(0, lax.div(live + 7, 8), slot_body, 0)
    out_ref[...] = acc[...].astype(BF)


def edge_backward(place, src, ang, own, other, rot, go, radial, wig_back):
    smem = pl.BlockSpec(memory_space=pltpu.SMEM)
    vmem = pl.BlockSpec(memory_space=VMEM)
    return pl.pallas_call(
        edge_kernel,
        out_shape=jax.ShapeDtypeStruct((16, PAD, C), BF),
        in_specs=[smem] * 3 + [vmem] * 6,
        out_specs=vmem,
        scratch_shapes=[
            VMEM((896, 1024), BF),
            VMEM((1536, 768), BF),
            VMEM((1280, 640), BF),
            VMEM((30 * 128, C), F32),
            VMEM((32 * 128, C), F32),
            VMEM((16, PAD, C), F32),
        ],
        compiler_params=pltpu.CompilerParams(vmem_limit_bytes=48 * 1024 * 1024),
    )(place, src, ang, own, other, rot, go, radial, wig_back)


def shift(value, axis, count, step):
    return lax.ppermute(value, axis, [(at, (at + step) % count) for at in range(count)])


def swap(value, axis):
    return lax.ppermute(value, axis, [(0, 1), (1, 0)])


def on_device(
    feat_in, ffn_in, grad_out, ffn_up, ffn_down, so2_zero, so2_one, so2_two, wigner,
    edge_src, edge_tgt, edge_angle, edge_radial, edge_count,
):
    core = lax.axis_index("core").astype(jnp.int32)
    y_lo = lax.axis_index("ylo").astype(jnp.int32)
    z_here = lax.axis_index("z").astype(jnp.int32)
    place = jnp.stack([core, y_lo, z_here, edge_count.reshape(())])

    own_pack = pack_own(place, so2_zero, so2_one, so2_two, feat_in)
    pair = pair_up(place, own_pack, swap(own_pack, "ylo"))
    up = [pair]
    down = [pair]
    for _ in range(3):
        up.append(shift(up[-1], "z", 8, 1))
        down.append(shift(down[-1], "z", 8, -1))
    half = PAIR_ROWS // 2
    far = jnp.concatenate([shift(up[3][:half], "z", 8, 1), shift(down[3][half:], "z", 8, -1)], axis=0)
    own = jnp.stack([pair, down[1], down[2], down[3], far, up[3], up[2], up[1]])
    other = swap(own, "core")

    target_grad = ffn_backward(ffn_in, grad_out, ffn_up, ffn_down)
    spread = jnp.broadcast_to(target_grad[None], (16, PAD, C))
    same_core = lax.all_to_all(spread, ("yhi", "x"), 0, 0, tiled=True)
    grads = jnp.concatenate([same_core, swap(same_core, "core")], axis=0)

    src_slots = edge_src.reshape(-1)
    tgt_slots = edge_tgt.reshape(-1)
    angle_slots = edge_angle.reshape(-1)
    feat = own[:, PAIR_FEAT:].reshape(16, PAD, C)
    src_piece = ((src_slots // 2 - z_here) % 8) * 2 + src_slots % 2
    tgt_piece = ((tgt_slots % 2) ^ core) * 16 + tgt_slots // 2
    wig = jnp.pad(wigner, ((0, 0), (0, 32 - KEEP), (0, PAD - COEF)))
    wig_back = jnp.transpose(wig, (0, 2, 1))
    rot, go = rotate_slots(src_piece, tgt_piece, angle_slots, feat, grads, wig)
    partial_sum = edge_backward(
        place, src_slots, angle_slots, own, other, rot, go, edge_radial.reshape(128, C), wig_back
    )
    parts = lax.all_to_all(partial_sum, ("z", "ylo"), 0, 0, tiled=True)
    total = target_grad.astype(F32) + jnp.sum(parts.astype(F32), axis=0)
    return total[None, :COEF].astype(BF)


def solution(mesh):
    devices = mesh.devices.reshape(4, 4, 2, 8, 2)
    fine = Mesh(devices, ("yhi", "x", "core", "z", "ylo"))
    src = ("yhi", "x", "core")
    tgt = ("z", "ylo")
    placed = (
        P(src + tgt, None, None),
        P(src + tgt, None, None),
        P(src + tgt, None, None),
        P(),
        P(),
        P(tgt, None),
        P(None, tgt, None),
        P(None, tgt, None),
        P(),
        P(src, tgt, None),
        P(src, tgt, None),
        P(src, tgt, None),
        P(src, tgt, None, None),
        P(src, tgt),
    )
    return jax.shard_map(
        on_device,
        mesh=fine,
        in_specs=placed,
        out_specs=P(src + tgt, None, None),
        check_vma=False,
    )
```

```python
import math

import jax
import jax.numpy as jnp
import numpy as np
from jax import lax
from jax.experimental import pallas as pl
from jax.experimental.pallas import tpu as pltpu
from jax.sharding import Mesh
from jax.sharding import PartitionSpec as P

LMAX = 6
GRID_SIDE = 14
C = 128
KEEP = 29
COEF = 49
PAD = 56
message_scale = 0.125
BF = jnp.bfloat16
F32 = jnp.float32
VMEM = pltpu.VMEM
SHARE = 192
SENT = 248
AT_ONE, AT_TWO, AT_MORE, WHOLE = 896, 1664, 2304, 3072


def sphere_tables(degree_max, grid_side):
    polar_angle = (np.arange(grid_side) + 0.5) * np.pi / grid_side
    azimuth = np.arange(grid_side) * 2.0 * np.pi / grid_side
    cosine = np.cos(polar_angle)
    sine_theta = np.sin(polar_angle)
    coef_count = (degree_max + 1) * (degree_max + 1)
    harmonics = np.zeros((grid_side, grid_side, coef_count))
    for order_m in range(degree_max + 1):
        diagonal = np.ones(grid_side)
        for factor in range(1, order_m + 1):
            diagonal = diagonal * (2 * factor - 1) * sine_theta
        legendre = {order_m: diagonal}
        if order_m + 1 <= degree_max:
            legendre[order_m + 1] = cosine * (2 * order_m + 1) * diagonal
        for degree in range(order_m + 2, degree_max + 1):
            legendre[degree] = (
                (2 * degree - 1) * cosine * legendre[degree - 1]
                - (degree + order_m - 1) * legendre[degree - 2]
            ) / (degree - order_m)
        for degree in range(order_m, degree_max + 1):
            scaling = math.sqrt(
                (2 * degree + 1)
                / (4.0 * math.pi)
                * math.factorial(degree - order_m)
                / math.factorial(degree + order_m)
            )
            if order_m > 0:
                scaling = scaling * math.sqrt(2.0)
            polar_part = scaling * legendre[degree]
            centre = degree * degree + degree
            harmonics[:, :, centre + order_m] = (
                polar_part[:, None] * np.cos(order_m * azimuth)[None, :]
            )
            if order_m > 0:
                harmonics[:, :, centre - order_m] = (
                    polar_part[:, None] * np.sin(order_m * azimuth)[None, :]
                )
    to_grid = harmonics.reshape(grid_side * grid_side, coef_count)
    quadrature = np.repeat(sine_theta * (np.pi / grid_side) * (2.0 * np.pi / grid_side), grid_side)
    from_grid = (to_grid * quadrature[:, None]).T
    return to_grid.astype(np.float32), from_grid.astype(np.float32)


def dot(left, right):
    return jnp.dot(left, right, preferred_element_type=F32)


def dot_nt(left, right):
    return lax.dot_general(left, right, (((1,), (1,)), ((), ())), preferred_element_type=F32)


def pack_kernel(place, zero_ref, one_ref, two_ref, feat_ref, out_ref):
    for share in range(8):

        @pl.when(place[2] == share)
        def _():
            out_ref[0, 0:56, :] = zero_ref[:, 128 * share : 128 * share + 128]
            side, block = divmod(share, 6)
            out_ref[0, 56:104, :] = one_ref[side, :, 128 * block : 128 * block + 128]
            side, block = divmod(share, 5)
            out_ref[0, 104:144, :] = two_ref[side, :, 128 * block : 128 * block + 128]
            if share < 4:
                out_ref[0, 144:192, :] = one_ref[1, :, 128 * (share + 2) : 128 * (share + 3)]
            elif share < 6:
                out_ref[0, 144:184, :] = two_ref[1, :, 128 * (share - 1) : 128 * share]
                out_ref[0, 184:192, :] = jnp.zeros((8, C), BF)
            else:
                out_ref[0, 144:192, :] = jnp.zeros((48, C), BF)

    out_ref[0, SHARE : SHARE + COEF, :] = feat_ref[0]
    out_ref[0, SHARE + COEF : SENT, :] = jnp.zeros((PAD - COEF, C), BF)
    for peer in range(1, 16):
        out_ref[peer] = out_ref[0]


def pack_own(place, so2_zero, so2_one, so2_two, feat_in):
    return pl.pallas_call(
        pack_kernel,
        out_shape=jax.ShapeDtypeStruct((16, SENT, C), BF),
        in_specs=[pl.BlockSpec(memory_space=pltpu.SMEM)] + [pl.BlockSpec(memory_space=VMEM)] * 4,
        out_specs=pl.BlockSpec(memory_space=VMEM),
    )(place, so2_zero, so2_one, so2_two, feat_in)


def join_kernel(place, own_ref, other_ref, whole_ref, half_ref, feat_ref):
    core = place[0]
    share = place[2]

    def fill(side, ref, this_share):
        def pair(z_row, first, rows):
            return jnp.concatenate(
                [
                    ref[2 * z_row, first : first + rows, :],
                    ref[2 * z_row + 1, first : first + rows, :],
                ],
                axis=0,
            )

        def put(z_row, start, first, rows):
            block = pair(z_row, first, rows)
            at = start + 2 * rows * z_row
            whole_ref[side, at : at + 2 * rows, :] = block
            at = start // 2 + 2 * rows * (z_row % 4)

            @pl.when(core == z_row // 4)
            def _():
                half_ref[side, at : at + 2 * rows, :] = block

        for z_row in range(8):
            put(z_row, 0, 0, 56)
            put(z_row, AT_ONE, 56, 48)
            put(z_row, AT_TWO, 104, 40)

        @pl.when(this_share < 4)
        def _():
            for z_row in range(8):
                put(z_row, AT_MORE, 144, 48)

        @pl.when((this_share >= 4) & (this_share < 6))
        def _():
            for z_row in range(8):
                put(z_row, AT_MORE, 144, 40)

        @pl.when((this_share >= 6))
        def _():
            whole_ref[side, AT_MORE:WHOLE, :] = jnp.zeros((WHOLE - AT_MORE, C), BF)
            half_ref[side, AT_MORE // 2 : WHOLE // 2, :] = jnp.zeros(((WHOLE - AT_MORE) // 2, C), BF)

        @pl.when((this_share >= 4) & (this_share < 6))
        def _():
            whole_ref[side, AT_MORE + 640 : WHOLE, :] = jnp.zeros((128, C), BF)
            half_ref[side, AT_MORE // 2 + 320 : WHOLE // 2, :] = jnp.zeros((64, C), BF)

    fill(0, own_ref, share)
    fill(1, other_ref, share + 1 - 2 * core)
    for peer in range(16):
        feat_ref[peer] = own_ref[peer, SHARE:SENT, :]


def join_shares(place, own, other):
    vmem = pl.BlockSpec(memory_space=VMEM)
    return pl.pallas_call(
        join_kernel,
        out_shape=(
            jax.ShapeDtypeStruct((2, WHOLE, C), BF),
            jax.ShapeDtypeStruct((2, WHOLE // 2, C), BF),
            jax.ShapeDtypeStruct((16, PAD, C), BF),
        ),
        in_specs=[pl.BlockSpec(memory_space=pltpu.SMEM), vmem, vmem],
        out_specs=(vmem,) * 3,
    )(place, own, other)


def ffn_kernel(x_ref, g_ref, up_ref, down_ref, to_ref, from_ref, back_ref, out_ref, xs, gs):
    xs[0:COEF, :] = x_ref[0]
    xs[COEF:PAD, :] = jnp.zeros((PAD - COEF, C), BF)
    gs[0:COEF, :] = g_ref[0]
    gs[COEF:PAD, :] = jnp.zeros((PAD - COEF, C), BF)
    grid_feat = dot(to_ref[...], xs[...]).astype(BF)
    grad_value = dot(from_ref[...], gs[...]).astype(BF)
    pre_act = dot(grid_feat, up_ref[...])
    grad_act = dot_nt(grad_value, down_ref[...])
    gate = jax.nn.sigmoid(pre_act)
    grad_pre = (grad_act * gate * (1.0 + pre_act * (1.0 - gate))).astype(BF)
    grad_grid = dot_nt(grad_pre, up_ref[...]).astype(BF)
    out_ref[...] = (gs[...].astype(F32) + dot(back_ref[...], grad_grid)).astype(BF)


def ffn_backward(ffn_in, grad_out, ffn_up, ffn_down):
    to_grid, from_grid = sphere_tables(LMAX, GRID_SIDE)
    points = to_grid.shape[0]
    to_pad = np.zeros((208, PAD), np.float32)
    to_pad[:points, :COEF] = to_grid
    from_pad = np.zeros((208, PAD), np.float32)
    from_pad[:points, :COEF] = from_grid.T
    back_pad = np.ascontiguousarray(to_pad.T)
    tables = [jnp.asarray(table, F32).astype(BF) for table in (to_pad, from_pad, back_pad)]
    return pl.pallas_call(
        ffn_kernel,
        out_shape=jax.ShapeDtypeStruct((PAD, C), BF),
        in_specs=[pl.BlockSpec(memory_space=VMEM)] * 7,
        out_specs=pl.BlockSpec(memory_space=VMEM),
        scratch_shapes=[VMEM((PAD, C), BF), VMEM((PAD, C), BF)],
    )(ffn_in, grad_out, ffn_up, ffn_down, *tables)


def rotate_kernel(src, tgt, ang, feat_ref, grad_ref, wig_ref, rot_ref, go_ref, acc):
    slots = 128

    def body(step, carry):
        for lane in range(8):
            slot = step * 8 + lane
            rows = jnp.concatenate([feat_ref[src[slot]], grad_ref[tgt[slot]]], axis=1)
            turned = dot(wig_ref[ang[slot]], rows)
            acc[pl.ds(slot, 32, stride=slots), :] = turned[:, :C]
            go_ref[pl.ds(slot, 32, stride=slots), :] = turned[:, C:]
        return carry

    lax.fori_loop(0, slots // 8, body, 0)
    rot_ref[...] = acc[...].astype(BF)


def rotate_slots(src, tgt, ang, feat, grads, wig):
    smem = pl.BlockSpec(memory_space=pltpu.SMEM)
    vmem = pl.BlockSpec(memory_space=VMEM)
    return pl.pallas_call(
        rotate_kernel,
        out_shape=(
            jax.ShapeDtypeStruct((32 * 128, C), BF),
            jax.ShapeDtypeStruct((32 * 128, C), F32),
        ),
        in_specs=[smem] * 3 + [vmem] * 3,
        out_specs=(vmem, vmem),
        scratch_shapes=[VMEM((32 * 128, C), F32)],
    )(src, tgt, ang, feat, grads, wig)


def edge_kernel(
    place, src, ang, own_ref, near_ref, far_ref, half_ref, half_far_ref,
    rot_ref, go_ref, radial_ref, wig_ref, out_ref,
    w_zero, w_one, w_two, hidden, grad_rot, acc,
):
    core = place[0]
    quarter = place[1]

    def take(ref, at, ahead, side, half):
        share = 2 * lax.rem(quarter + ahead, 4) + side
        cut = 1 if half is None else 2

        def move(weight, block, first, rows):
            rows = rows // cut
            start = 0 if half is None else pl.multiple_of(rows * half, 64)
            weight[block, pl.ds(start, rows), :] = ref[at, first // cut : first // cut + rows, :]

        move(w_zero, share, 0, 896)
        move(w_one, share, AT_ONE, 768)
        move(w_two, share, AT_TWO, 640)

        @pl.when(share < 4)
        def _():
            move(w_one, 8 + share, AT_MORE, 768)

        @pl.when((share >= 4) & (share < 6))
        def _():
            move(w_two, 4 + share, AT_MORE, 640)

    for at in range(2):
        side = core if at == 0 else 1 - core
        take(own_ref, at, 0, side, None)
        take(near_ref, at, 3 - 2 * core, side, None)
        take(far_ref, at, 1 + 2 * core, 1 - side, None)
        take(half_ref, at, 2, side, core)
        take(half_far_ref, at, 2, 1 - side, 1 - core)

    def columns(weight, first, count, rows):
        return jnp.concatenate([weight[first + at, rows, :] for at in range(count)], axis=1)

    every = slice(None)

    def turned(first, count):
        return jnp.concatenate(
            [rot_ref[128 * row : 128 * row + 128, :] for row in range(first, first + count)], axis=1
        )

    radial = radial_ref[...].astype(F32)

    def put(first, rows, value):
        for row in range(rows):
            hidden[128 * (first + row) : 128 * (first + row) + 128, :] = (
                value[:, 128 * row : 128 * row + 128] * radial
            )

    left = turned(0, 7)
    for pair in range(4):
        put(2 * pair, 2, dot(left, columns(w_zero, 2 * pair, 2, every)))

    def higher(first, count, weight, hidden_first):
        plus = turned(first, count)
        minus = turned(first + count, count)
        both = jnp.concatenate(
            [jnp.concatenate([plus, -minus], axis=1), jnp.concatenate([minus, plus], axis=1)], axis=0
        )
        start = 0
        while start < count:
            wide = min(2, count - start)
            value = dot(
                both,
                jnp.concatenate(
                    [columns(weight, start, wide, every), columns(weight, count + start, wide, every)],
                    axis=0,
                ),
            )
            put(hidden_first + start, wide, value[:128])
            put(hidden_first + count + start, wide, value[128:])
            start = start + wide

    higher(7, 6, w_one, 8)
    higher(19, 5, w_two, 20)

    def hid(row):
        return hidden[128 * row : 128 * row + 128, :]

    def go(row):
        return go_ref[128 * row : 128 * row + 128, :] * message_scale

    scalar_pre = hid(0)
    sigmoid_scalar = jax.nn.sigmoid(scalar_pre)
    sigmoid_gate = jax.nn.sigmoid(hid(7))
    weight_gate = sigmoid_gate * radial
    grads = {}
    grads[0] = (
        go(0) * sigmoid_scalar * (1.0 + scalar_pre * (1.0 - sigmoid_scalar)) * radial
    ).astype(BF)
    total = jnp.zeros((128, C), F32)
    for kept in range(1, KEEP):
        row = kept if kept < 7 else kept + 1
        value = go(kept)
        total = total + value * hid(row)
        grads[row] = (value * weight_gate).astype(BF)
    grads[7] = (total * sigmoid_gate * (1.0 - sigmoid_gate) * radial).astype(BF)

    def side_by_side(first, count):
        return jnp.concatenate([grads[row] for row in range(first, first + count)], axis=1)

    def keep(first, value):
        for row in range(value.shape[1] // 128):
            grad_rot[128 * (first + row) : 128 * (first + row) + 128, :] = value[
                :, 128 * row : 128 * row + 128
            ]

    right = side_by_side(0, 8)
    for start in (0, 2, 4, 6):
        wide = min(2, 7 - start)
        rows = slice(128 * start, 128 * (start + wide))
        keep(start, dot_nt(right, columns(w_zero, 0, 8, rows)))

    def back(first, count, weight, hidden_first):
        both = jnp.concatenate(
            [side_by_side(hidden_first, count), side_by_side(hidden_first + count, count)], axis=0
        )
        start = 0
        while start < count:
            wide = min(2, count - start)
            rows = slice(128 * start, 128 * (start + wide))
            real = dot_nt(both, columns(weight, 0, count, rows))
            imag = dot_nt(both, columns(weight, count, count, rows))
            keep(first + start, real[:128] + imag[128:])
            keep(first + count + start, real[128:] - imag[:128])
            start = start + wide

    back(7, 6, w_one, 8)
    back(19, 5, w_two, 20)
    grad_rot[KEEP * 128 :, :] = jnp.zeros((3 * 128, C), F32)

    acc[...] = jnp.zeros_like(acc)
    live = place[3]

    def slot_body(step, carry):
        for lane in range(8):
            slot = step * 8 + lane
            rows = grad_rot[pl.ds(slot, 32, stride=128), :]
            rows = jnp.where(slot < live, rows, 0.0).astype(BF)
            acc[src[slot]] += dot(wig_ref[ang[slot]], rows)
        return carry

    lax.fori_loop(0, lax.div(live + 7, 8), slot_body, 0)
    out_ref[...] = acc[...].astype(BF)


def edge_backward(place, src, ang, shares, rot, go, radial, wig_back):
    smem = pl.BlockSpec(memory_space=pltpu.SMEM)
    vmem = pl.BlockSpec(memory_space=VMEM)
    return pl.pallas_call(
        edge_kernel,
        out_shape=jax.ShapeDtypeStruct((16, PAD, C), BF),
        in_specs=[smem] * 3 + [vmem] * 9,
        out_specs=vmem,
        scratch_shapes=[
            VMEM((8, 896, C), BF),
            VMEM((12, 768, C), BF),
            VMEM((10, 640, C), BF),
            VMEM((30 * 128, C), F32),
            VMEM((32 * 128, C), F32),
            VMEM((16, PAD, C), F32),
        ],
        compiler_params=pltpu.CompilerParams(vmem_limit_bytes=48 * 1024 * 1024),
    )(place, src, ang, *shares, rot, go, radial, wig_back)


def swap(value, axis):
    return lax.ppermute(value, axis, [(0, 1), (1, 0)])


def body(
    feat_in, ffn_in, grad_out, ffn_up, ffn_down, so2_zero, so2_one, so2_two, wigner,
    edge_src, edge_tgt, edge_angle, edge_radial, edge_count,
):
    core = lax.axis_index("core").astype(jnp.int32)
    x_here = lax.axis_index("x").astype(jnp.int32)
    y_hi = lax.axis_index("yhi").astype(jnp.int32)
    quarter = (x_here + 2 * y_hi) % 4
    place = jnp.stack([core, quarter, 2 * quarter + core, edge_count.reshape(())])

    sent = pack_own(place, so2_zero, so2_one, so2_two, feat_in)
    got = lax.all_to_all(sent, ("z", "ylo"), 0, 0, tiled=True)
    target_grad = ffn_backward(ffn_in, grad_out, ffn_up, ffn_down)
    grads = target_grad[None]
    for axis, mask in (("yhi", 2), ("yhi", 1), ("x", 2), ("x", 1), ("core", 1)):
        count = 2 if axis == "core" else 4
        other = lax.ppermute(grads, axis, [(at, at ^ mask) for at in range(count)])
        grads = jnp.concatenate([grads, other], axis=0)
    got_other = swap(got, "core")
    own, half, feat = join_shares(place, got, got_other)
    turn = [(2 * at, 2 * ((at + 1) % 4)) for at in range(4)]
    turn = turn + [(2 * at + 1, 2 * ((at + 3) % 4) + 1) for at in range(4)]
    near = lax.ppermute(own, ("x", "core"), turn)
    half_near = lax.ppermute(half, ("yhi", "core"), turn)
    far = swap(near, "core")
    half_far = swap(half_near, "core")
    shares = (own, near, far, half_near, half_far)

    src_slots = edge_src.reshape(-1)
    tgt_slots = edge_tgt.reshape(-1)
    angle_slots = edge_angle.reshape(-1)
    y_turn = (tgt_slots // 8) ^ y_hi
    x_turn = (tgt_slots // 2 % 4) ^ x_here
    core_turn = (tgt_slots % 2) ^ core
    tgt_piece = core_turn * 16 + x_turn % 2 * 8 + x_turn // 2 * 4 + y_turn % 2 * 2 + y_turn // 2
    wig = jnp.pad(wigner, ((0, 0), (0, 32 - KEEP), (0, PAD - COEF)))
    wig_back = jnp.transpose(wig, (0, 2, 1))
    rot, go = rotate_slots(src_slots, tgt_piece, angle_slots, feat, grads, wig)
    partial_sum = edge_backward(
        place, src_slots, angle_slots, shares, rot, go, edge_radial.reshape(128, C), wig_back
    )
    parts = lax.all_to_all(partial_sum, ("z", "ylo"), 0, 0, tiled=True)
    total = target_grad.astype(F32) + jnp.sum(parts.astype(F32), axis=0)
    return total[None, :COEF].astype(BF)


def solution(mesh):
    devices = mesh.devices.reshape(4, 4, 2, 8, 2)
    fine = Mesh(devices, ("yhi", "x", "core", "z", "ylo"))
    src = ("yhi", "x", "core")
    tgt = ("z", "ylo")
    placed = (
        P(src + tgt, None, None),
        P(src + tgt, None, None),
        P(src + tgt, None, None),
        P(),
        P(),
        P(tgt, None),
        P(None, tgt, None),
        P(None, tgt, None),
        P(),
        P(src, tgt, None),
        P(src, tgt, None),
        P(src, tgt, None),
        P(src, tgt, None, None),
        P(src, tgt),
    )
    return jax.shard_map(
        body,
        mesh=fine,
        in_specs=placed,
        out_specs=P(src + tgt, None, None),
        check_vma=False,
    )
```

```python
import math

import jax
import jax.numpy as jnp
import numpy as np
from jax import lax
from jax.experimental import pallas as pl
from jax.experimental.pallas import tpu as pltpu
from jax.sharding import Mesh
from jax.sharding import PartitionSpec as P

LMAX = 6
GRID_SIDE = 14
C = 128
KEEP = 29
COEF = 49
PAD = 56
message_scale = 0.125
BF = jnp.bfloat16
F32 = jnp.float32
VMEM = pltpu.VMEM
SHARE = 192
SENT = 248
AT_ONE, AT_TWO, AT_MORE, WHOLE = 896, 1664, 2304, 3072


def sphere_tables(degree_max, grid_side):
    polar_angle = (np.arange(grid_side) + 0.5) * np.pi / grid_side
    azimuth = np.arange(grid_side) * 2.0 * np.pi / grid_side
    cosine = np.cos(polar_angle)
    sine_theta = np.sin(polar_angle)
    coef_count = (degree_max + 1) * (degree_max + 1)
    harmonics = np.zeros((grid_side, grid_side, coef_count))
    for order_m in range(degree_max + 1):
        diagonal = np.ones(grid_side)
        for factor in range(1, order_m + 1):
            diagonal = diagonal * (2 * factor - 1) * sine_theta
        legendre = {order_m: diagonal}
        if order_m + 1 <= degree_max:
            legendre[order_m + 1] = cosine * (2 * order_m + 1) * diagonal
        for degree in range(order_m + 2, degree_max + 1):
            legendre[degree] = (
                (2 * degree - 1) * cosine * legendre[degree - 1]
                - (degree + order_m - 1) * legendre[degree - 2]
            ) / (degree - order_m)
        for degree in range(order_m, degree_max + 1):
            scaling = math.sqrt(
                (2 * degree + 1)
                / (4.0 * math.pi)
                * math.factorial(degree - order_m)
                / math.factorial(degree + order_m)
            )
            if order_m > 0:
                scaling = scaling * math.sqrt(2.0)
            polar_part = scaling * legendre[degree]
            centre = degree * degree + degree
            harmonics[:, :, centre + order_m] = (
                polar_part[:, None] * np.cos(order_m * azimuth)[None, :]
            )
            if order_m > 0:
                harmonics[:, :, centre - order_m] = (
                    polar_part[:, None] * np.sin(order_m * azimuth)[None, :]
                )
    to_grid = harmonics.reshape(grid_side * grid_side, coef_count)
    quadrature = np.repeat(sine_theta * (np.pi / grid_side) * (2.0 * np.pi / grid_side), grid_side)
    from_grid = (to_grid * quadrature[:, None]).T
    return to_grid.astype(np.float32), from_grid.astype(np.float32)


def grant(mebibytes):
    return pltpu.CompilerParams(vmem_limit_bytes=mebibytes * 1024 * 1024)


def dot(left, right):
    return jnp.dot(left, right, preferred_element_type=F32)


def dot_nt(left, right):
    return lax.dot_general(left, right, (((1,), (1,)), ((), ())), preferred_element_type=F32)


def pack_kernel(place, zero_ref, one_ref, two_ref, feat_ref, x_ref, g_ref, out_ref, pair_ref):
    for row, ref in ((0, x_ref), (1, g_ref)):
        pair_ref[row, 0:COEF, :] = ref[0]
        pair_ref[row, COEF:PAD, :] = jnp.zeros((PAD - COEF, C), BF)

    for share in range(8):

        @pl.when(place[2] == share)
        def _():
            out_ref[0, 0:56, :] = zero_ref[:, 128 * share : 128 * share + 128]
            side, block = divmod(share, 6)
            out_ref[0, 56:104, :] = one_ref[side, :, 128 * block : 128 * block + 128]
            side, block = divmod(share, 5)
            out_ref[0, 104:144, :] = two_ref[side, :, 128 * block : 128 * block + 128]
            if share < 4:
                out_ref[0, 144:192, :] = one_ref[1, :, 128 * (share + 2) : 128 * (share + 3)]
            elif share < 6:
                out_ref[0, 144:184, :] = two_ref[1, :, 128 * (share - 1) : 128 * share]
                out_ref[0, 184:192, :] = jnp.zeros((8, C), BF)
            else:
                out_ref[0, 144:192, :] = jnp.zeros((48, C), BF)

    out_ref[0, SHARE : SHARE + COEF, :] = feat_ref[0]
    out_ref[0, SHARE + COEF : SENT, :] = jnp.zeros((PAD - COEF, C), BF)
    for peer in range(1, 16):
        out_ref[peer] = out_ref[0]


def pack_own(place, so2_zero, so2_one, so2_two, feat_in, ffn_in, grad_out):
    vmem = pl.BlockSpec(memory_space=VMEM)
    return pl.pallas_call(
        pack_kernel,
        out_shape=(
            jax.ShapeDtypeStruct((16, SENT, C), BF),
            jax.ShapeDtypeStruct((2, PAD, C), BF),
        ),
        in_specs=[pl.BlockSpec(memory_space=pltpu.SMEM)] + [vmem] * 6,
        out_specs=(vmem, vmem),
        compiler_params=grant(16),
    )(place, so2_zero, so2_one, so2_two, feat_in, ffn_in, grad_out)


def join_kernel(place, own_ref, other_ref, whole_ref, half_ref, feat_ref):
    core = place[0]
    share = place[2]

    def fill(side, ref, this_share):
        def pair(z_row, first, rows):
            return jnp.concatenate(
                [
                    ref[2 * z_row, first : first + rows, :],
                    ref[2 * z_row + 1, first : first + rows, :],
                ],
                axis=0,
            )

        def put(z_row, start, first, rows):
            block = pair(z_row, first, rows)
            at = start + 2 * rows * z_row
            whole_ref[side, at : at + 2 * rows, :] = block
            at = start // 2 + 2 * rows * (z_row % 4)

            @pl.when(core == z_row // 4)
            def _():
                half_ref[side, at : at + 2 * rows, :] = block

        for z_row in range(8):
            put(z_row, 0, 0, 56)
            put(z_row, AT_ONE, 56, 48)
            put(z_row, AT_TWO, 104, 40)

        @pl.when(this_share < 4)
        def _():
            for z_row in range(8):
                put(z_row, AT_MORE, 144, 48)

        @pl.when((this_share >= 4) & (this_share < 6))
        def _():
            for z_row in range(8):
                put(z_row, AT_MORE, 144, 40)

        @pl.when((this_share >= 6))
        def _():
            whole_ref[side, AT_MORE:WHOLE, :] = jnp.zeros((WHOLE - AT_MORE, C), BF)
            half_ref[side, AT_MORE // 2 : WHOLE // 2, :] = jnp.zeros(((WHOLE - AT_MORE) // 2, C), BF)

        @pl.when((this_share >= 4) & (this_share < 6))
        def _():
            whole_ref[side, AT_MORE + 640 : WHOLE, :] = jnp.zeros((128, C), BF)
            half_ref[side, AT_MORE // 2 + 320 : WHOLE // 2, :] = jnp.zeros((64, C), BF)

    fill(0, own_ref, share)
    fill(1, other_ref, share + 1 - 2 * core)
    for peer in range(16):
        feat_ref[peer] = own_ref[peer, SHARE:SENT, :]


def join_shares(place, own, other):
    vmem = pl.BlockSpec(memory_space=VMEM)
    return pl.pallas_call(
        join_kernel,
        out_shape=(
            jax.ShapeDtypeStruct((2, WHOLE, C), BF),
            jax.ShapeDtypeStruct((2, WHOLE // 2, C), BF),
            jax.ShapeDtypeStruct((16, PAD, C), BF),
        ),
        in_specs=[pl.BlockSpec(memory_space=pltpu.SMEM), vmem, vmem],
        out_specs=(vmem,) * 3,
        compiler_params=grant(16),
    )(place, own, other)


def ffn_kernel(own_ref, other_ref, up_ref, down_ref, to_ref, from_ref, back_ref, spread_ref):
    for place, ref in ((0, own_ref), (1, other_ref)):
        grid_feat = dot(to_ref[...], ref[0]).astype(BF)
        grad_value = dot(from_ref[...], ref[1]).astype(BF)
        pre_act = dot(grid_feat, up_ref[...])
        grad_act = dot_nt(grad_value, down_ref[...])
        gate = jax.nn.sigmoid(pre_act)
        grad_pre = (grad_act * gate * (1.0 + pre_act * (1.0 - gate))).astype(BF)
        grad_grid = dot_nt(grad_pre, up_ref[...]).astype(BF)
        result = (ref[1].astype(F32) + dot(back_ref[...], grad_grid)).astype(BF)
        for peer in range(16):
            spread_ref[peer, place] = result


def ffn_backward(own, other, ffn_up, ffn_down):
    to_grid, from_grid = sphere_tables(LMAX, GRID_SIDE)
    points = to_grid.shape[0]
    to_pad = np.zeros((208, PAD), np.float32)
    to_pad[:points, :COEF] = to_grid
    from_pad = np.zeros((208, PAD), np.float32)
    from_pad[:points, :COEF] = from_grid.T
    back_pad = np.ascontiguousarray(to_pad.T)
    tables = [jnp.asarray(table, F32).astype(BF) for table in (to_pad, from_pad, back_pad)]
    return pl.pallas_call(
        ffn_kernel,
        out_shape=jax.ShapeDtypeStruct((16, 2, PAD, C), BF),
        in_specs=[pl.BlockSpec(memory_space=VMEM)] * 7,
        out_specs=pl.BlockSpec(memory_space=VMEM),
        compiler_params=grant(16),
    )(own, other, ffn_up, ffn_down, *tables)


def rotate_kernel(src, tgt, ang, feat_ref, grad_ref, wig_ref, rot_ref, go_ref, acc):
    slots = 128

    def body(step, carry):
        for lane in range(8):
            slot = step * 8 + lane
            rows = jnp.concatenate([feat_ref[src[slot]], grad_ref[tgt[slot]]], axis=1)
            turned = dot(wig_ref[ang[slot]], rows)
            acc[pl.ds(slot, 32, stride=slots), :] = turned[:, :C]
            go_ref[pl.ds(slot, 32, stride=slots), :] = turned[:, C:]
        return carry

    lax.fori_loop(0, slots // 8, body, 0)
    rot_ref[...] = acc[...].astype(BF)


def rotate_slots(src, tgt, ang, feat, grads, wig):
    smem = pl.BlockSpec(memory_space=pltpu.SMEM)
    vmem = pl.BlockSpec(memory_space=VMEM)
    return pl.pallas_call(
        rotate_kernel,
        out_shape=(
            jax.ShapeDtypeStruct((32 * 128, C), BF),
            jax.ShapeDtypeStruct((32 * 128, C), F32),
        ),
        in_specs=[smem] * 3 + [vmem] * 3,
        out_specs=(vmem, vmem),
        scratch_shapes=[VMEM((32 * 128, C), F32)],
        compiler_params=grant(16),
    )(src, tgt, ang, feat, grads, wig)


def edge_kernel(
    place, src, ang, own_ref, near_ref, far_ref, half_ref, half_far_ref,
    rot_ref, go_ref, radial_ref, wig_ref, out_ref,
    w_zero, w_one, w_two, hidden, grad_rot, acc, sems,
):
    core = place[0]
    quarter = place[1]
    copies = ([], [], [])

    def take(number, ref, at, ahead, side, half):
        share = 2 * lax.rem(quarter + ahead, 4) + side
        cut = 1 if half is None else 2

        def move(weight, block, first, rows, part):
            rows = rows // cut
            start = 0 if half is None else pl.multiple_of(rows * half, 64)
            return pltpu.make_async_copy(
                ref.at[at, pl.ds(first // cut, rows), :],
                weight.at[block, pl.ds(start, rows), :],
                sems.at[number, part],
            )

        extra_one = share < 4
        extra_two = (share >= 4) & (share < 6)
        copies[0].append((None, lambda: move(w_zero, share, 0, 896, 0)))
        copies[1].append((None, lambda: move(w_one, share, AT_ONE, 768, 1)))
        copies[2].append((None, lambda: move(w_two, share, AT_TWO, 640, 2)))
        copies[1].append((extra_one, lambda: move(w_one, 8 + share, AT_MORE, 768, 3)))
        copies[2].append((extra_two, lambda: move(w_two, 4 + share, AT_MORE, 640, 3)))

    number = 0
    for at in range(2):
        side = core if at == 0 else 1 - core
        for ref, ahead, its_side, half in (
            (own_ref, 0, side, None),
            (near_ref, 3 - 2 * core, side, None),
            (far_ref, 1 + 2 * core, 1 - side, None),
            (half_ref, 2, side, core),
            (half_far_ref, 2, 1 - side, 1 - core),
        ):
            take(number, ref, at, ahead, its_side, half)
            number = number + 1

    def each(group, act):
        for condition, make in copies[group]:
            if condition is None:
                act(make())
            else:
                pl.when(condition)(lambda make=make: act(make()))

    for group in range(3):
        each(group, lambda copy: copy.start())

    def columns(weight, first, count, rows):
        return jnp.concatenate([weight[first + at, rows, :] for at in range(count)], axis=1)

    every = slice(None)

    def turned(first, count):
        return jnp.concatenate(
            [rot_ref[128 * row : 128 * row + 128, :] for row in range(first, first + count)], axis=1
        )

    radial = radial_ref[...].astype(F32)

    def put(first, rows, value):
        for row in range(rows):
            hidden[128 * (first + row) : 128 * (first + row) + 128, :] = (
                value[:, 128 * row : 128 * row + 128] * radial
            )

    each(0, lambda copy: copy.wait())
    left = turned(0, 7)
    for pair in range(4):
        put(2 * pair, 2, dot(left, columns(w_zero, 2 * pair, 2, every)))

    def higher(first, count, weight, hidden_first):
        plus = turned(first, count)
        minus = turned(first + count, count)
        both = jnp.concatenate(
            [jnp.concatenate([plus, -minus], axis=1), jnp.concatenate([minus, plus], axis=1)], axis=0
        )
        start = 0
        while start < count:
            wide = min(2, count - start)
            value = dot(
                both,
                jnp.concatenate(
                    [columns(weight, start, wide, every), columns(weight, count + start, wide, every)],
                    axis=0,
                ),
            )
            put(hidden_first + start, wide, value[:128])
            put(hidden_first + count + start, wide, value[128:])
            start = start + wide

    each(1, lambda copy: copy.wait())
    higher(7, 6, w_one, 8)
    each(2, lambda copy: copy.wait())
    higher(19, 5, w_two, 20)

    def hid(row):
        return hidden[128 * row : 128 * row + 128, :]

    def go(row):
        return go_ref[128 * row : 128 * row + 128, :] * message_scale

    scalar_pre = hid(0)
    sigmoid_scalar = jax.nn.sigmoid(scalar_pre)
    sigmoid_gate = jax.nn.sigmoid(hid(7))
    weight_gate = sigmoid_gate * radial
    grads = {}
    grads[0] = (
        go(0) * sigmoid_scalar * (1.0 + scalar_pre * (1.0 - sigmoid_scalar)) * radial
    ).astype(BF)
    total = jnp.zeros((128, C), F32)
    for kept in range(1, KEEP):
        row = kept if kept < 7 else kept + 1
        value = go(kept)
        total = total + value * hid(row)
        grads[row] = (value * weight_gate).astype(BF)
    grads[7] = (total * sigmoid_gate * (1.0 - sigmoid_gate) * radial).astype(BF)

    def side_by_side(first, count):
        return jnp.concatenate([grads[row] for row in range(first, first + count)], axis=1)

    def keep(first, value):
        for row in range(value.shape[1] // 128):
            grad_rot[128 * (first + row) : 128 * (first + row) + 128, :] = value[
                :, 128 * row : 128 * row + 128
            ]

    right = side_by_side(0, 8)
    for start in (0, 2, 4, 6):
        wide = min(2, 7 - start)
        rows = slice(128 * start, 128 * (start + wide))
        keep(start, dot_nt(right, columns(w_zero, 0, 8, rows)))

    def back(first, count, weight, hidden_first):
        both = jnp.concatenate(
            [side_by_side(hidden_first, count), side_by_side(hidden_first + count, count)], axis=0
        )
        start = 0
        while start < count:
            wide = min(2, count - start)
            rows = slice(128 * start, 128 * (start + wide))
            real = dot_nt(both, columns(weight, 0, count, rows))
            imag = dot_nt(both, columns(weight, count, count, rows))
            keep(first + start, real[:128] + imag[128:])
            keep(first + count + start, real[128:] - imag[:128])
            start = start + wide

    back(7, 6, w_one, 8)
    back(19, 5, w_two, 20)
    grad_rot[KEEP * 128 :, :] = jnp.zeros((3 * 128, C), F32)

    acc[...] = jnp.zeros_like(acc)
    live = place[3]

    def slot_body(step, carry):
        for lane in range(8):
            slot = step * 8 + lane
            rows = grad_rot[pl.ds(slot, 32, stride=128), :]
            rows = jnp.where(slot < live, rows, 0.0).astype(BF)
            acc[src[slot]] += dot(wig_ref[ang[slot]], rows)
        return carry

    lax.fori_loop(0, lax.div(live + 7, 8), slot_body, 0)
    out_ref[...] = acc[...].astype(BF)


def edge_backward(place, src, ang, shares, rot, go, radial, wig_back):
    smem = pl.BlockSpec(memory_space=pltpu.SMEM)
    vmem = pl.BlockSpec(memory_space=VMEM)
    return pl.pallas_call(
        edge_kernel,
        out_shape=jax.ShapeDtypeStruct((16, PAD, C), BF),
        in_specs=[smem] * 3 + [pl.BlockSpec(memory_space=pl.ANY)] * 5 + [vmem] * 4,
        out_specs=vmem,
        scratch_shapes=[
            VMEM((8, 896, C), BF),
            VMEM((12, 768, C), BF),
            VMEM((10, 640, C), BF),
            VMEM((30 * 128, C), F32),
            VMEM((32 * 128, C), F32),
            VMEM((16, PAD, C), F32),
            pltpu.SemaphoreType.DMA((10, 4)),
        ],
        compiler_params=grant(28),
    )(place, src, ang, *shares, rot, go, radial, wig_back)


def swap(value, axis):
    return lax.ppermute(value, axis, [(0, 1), (1, 0)])


def body(
    feat_in, ffn_in, grad_out, ffn_up, ffn_down, so2_zero, so2_one, so2_two, wigner,
    edge_src, edge_tgt, edge_angle, edge_radial, edge_count,
):
    core = lax.axis_index("core").astype(jnp.int32)
    x_here = lax.axis_index("x").astype(jnp.int32)
    y_hi = lax.axis_index("yhi").astype(jnp.int32)
    quarter = (x_here + 2 * y_hi) % 4
    place = jnp.stack([core, quarter, 2 * quarter + core, edge_count.reshape(())])

    sent, pair = pack_own(place, so2_zero, so2_one, so2_two, feat_in, ffn_in, grad_out)
    pair_other = swap(pair, "core")
    got = lax.all_to_all(sent, ("z", "ylo"), 0, 0, tiled=True)
    spread = ffn_backward(pair, pair_other, ffn_up, ffn_down)
    grads = lax.all_to_all(spread, ("yhi", "x"), 0, 0, tiled=True)
    grads = grads.reshape(32, PAD, C)
    got_other = swap(got, "core")
    own, half, feat = join_shares(place, got, got_other)
    turn = [(2 * at, 2 * ((at + 1) % 4)) for at in range(4)]
    turn = turn + [(2 * at + 1, 2 * ((at + 3) % 4) + 1) for at in range(4)]
    near = lax.ppermute(own, ("x", "core"), turn)
    half_near = lax.ppermute(half, ("yhi", "core"), turn)
    far = swap(near, "core")
    half_far = swap(half_near, "core")
    shares = (own, near, far, half_near, half_far)

    src_slots = edge_src.reshape(-1)
    tgt_slots = edge_tgt.reshape(-1)
    angle_slots = edge_angle.reshape(-1)
    tgt_piece = tgt_slots // 2 * 2 + ((tgt_slots % 2) ^ core)
    wig = jnp.pad(wigner, ((0, 0), (0, 32 - KEEP), (0, PAD - COEF)))
    wig_back = jnp.transpose(wig, (0, 2, 1))
    rot, go = rotate_slots(src_slots, tgt_piece, angle_slots, feat, grads, wig)
    partial_sum = edge_backward(
        place, src_slots, angle_slots, shares, rot, go, edge_radial.reshape(128, C), wig_back
    )
    parts = lax.all_to_all(partial_sum, ("z", "ylo"), 0, 0, tiled=True)
    total = spread[0, 0].astype(F32) + jnp.sum(parts.astype(F32), axis=0)
    return total[None, :COEF].astype(BF)


def solution(mesh):
    devices = mesh.devices.reshape(4, 4, 2, 8, 2)
    fine = Mesh(devices, ("yhi", "x", "core", "z", "ylo"))
    src = ("yhi", "x", "core")
    tgt = ("z", "ylo")
    placed = (
        P(src + tgt, None, None),
        P(src + tgt, None, None),
        P(src + tgt, None, None),
        P(),
        P(),
        P(tgt, None),
        P(None, tgt, None),
        P(None, tgt, None),
        P(),
        P(src, tgt, None),
        P(src, tgt, None),
        P(src, tgt, None),
        P(src, tgt, None, None),
        P(src, tgt),
    )
    return jax.shard_map(
        body,
        mesh=fine,
        in_specs=placed,
        out_specs=P(src + tgt, None, None),
        check_vma=False,
    )
```

```python
import math

import jax
import jax.numpy as jnp
import numpy as np
from jax import lax
from jax.experimental import pallas as pl
from jax.experimental.pallas import tpu as pltpu
from jax.sharding import Mesh
from jax.sharding import PartitionSpec as P

LMAX = 6
GRID_SIDE = 14
C = 128
KEEP = 29
COEF = 49
PAD = 56
message_scale = 0.125
BF = jnp.bfloat16
F32 = jnp.float32
VMEM = pltpu.VMEM
SHARE = 192
SENT = 248
AT_ONE, AT_TWO, AT_MORE, WHOLE = 896, 1664, 2304, 3072


def sphere_tables(degree_max, grid_side):
    polar_angle = (np.arange(grid_side) + 0.5) * np.pi / grid_side
    azimuth = np.arange(grid_side) * 2.0 * np.pi / grid_side
    cosine = np.cos(polar_angle)
    sine_theta = np.sin(polar_angle)
    coef_count = (degree_max + 1) * (degree_max + 1)
    harmonics = np.zeros((grid_side, grid_side, coef_count))
    for order_m in range(degree_max + 1):
        diagonal = np.ones(grid_side)
        for factor in range(1, order_m + 1):
            diagonal = diagonal * (2 * factor - 1) * sine_theta
        legendre = {order_m: diagonal}
        if order_m + 1 <= degree_max:
            legendre[order_m + 1] = cosine * (2 * order_m + 1) * diagonal
        for degree in range(order_m + 2, degree_max + 1):
            legendre[degree] = (
                (2 * degree - 1) * cosine * legendre[degree - 1]
                - (degree + order_m - 1) * legendre[degree - 2]
            ) / (degree - order_m)
        for degree in range(order_m, degree_max + 1):
            scaling = math.sqrt(
                (2 * degree + 1)
                / (4.0 * math.pi)
                * math.factorial(degree - order_m)
                / math.factorial(degree + order_m)
            )
            if order_m > 0:
                scaling = scaling * math.sqrt(2.0)
            polar_part = scaling * legendre[degree]
            centre = degree * degree + degree
            harmonics[:, :, centre + order_m] = (
                polar_part[:, None] * np.cos(order_m * azimuth)[None, :]
            )
            if order_m > 0:
                harmonics[:, :, centre - order_m] = (
                    polar_part[:, None] * np.sin(order_m * azimuth)[None, :]
                )
    to_grid = harmonics.reshape(grid_side * grid_side, coef_count)
    quadrature = np.repeat(sine_theta * (np.pi / grid_side) * (2.0 * np.pi / grid_side), grid_side)
    from_grid = (to_grid * quadrature[:, None]).T
    return to_grid.astype(np.float32), from_grid.astype(np.float32)


def grant(mebibytes):
    return pltpu.CompilerParams(vmem_limit_bytes=mebibytes * 1024 * 1024)


def dot(left, right):
    return jnp.dot(left, right, preferred_element_type=F32)


def dot_nt(left, right):
    return lax.dot_general(left, right, (((1,), (1,)), ((), ())), preferred_element_type=F32)


def pack_kernel(place, zero_ref, one_ref, two_ref, feat_ref, x_ref, g_ref, out_ref, pair_ref):
    for row, ref in ((0, x_ref), (1, g_ref)):
        pair_ref[row, 0:COEF, :] = ref[0]
        pair_ref[row, COEF:PAD, :] = jnp.zeros((PAD - COEF, C), BF)

    for share in range(8):

        @pl.when(place[2] == share)
        def _():
            out_ref[0, 0:56, :] = zero_ref[:, 128 * share : 128 * share + 128]
            side, block = divmod(share, 6)
            out_ref[0, 56:104, :] = one_ref[side, :, 128 * block : 128 * block + 128]
            side, block = divmod(share, 5)
            out_ref[0, 104:144, :] = two_ref[side, :, 128 * block : 128 * block + 128]
            if share < 4:
                out_ref[0, 144:192, :] = one_ref[1, :, 128 * (share + 2) : 128 * (share + 3)]
            elif share < 6:
                out_ref[0, 144:184, :] = two_ref[1, :, 128 * (share - 1) : 128 * share]
                out_ref[0, 184:192, :] = jnp.zeros((8, C), BF)
            else:
                out_ref[0, 144:192, :] = jnp.zeros((48, C), BF)

    out_ref[0, SHARE : SHARE + COEF, :] = feat_ref[0]
    out_ref[0, SHARE + COEF : SENT, :] = jnp.zeros((PAD - COEF, C), BF)
    for peer in range(1, 16):
        out_ref[peer] = out_ref[0]


def pack_own(place, so2_zero, so2_one, so2_two, feat_in, ffn_in, grad_out):
    vmem = pl.BlockSpec(memory_space=VMEM)
    return pl.pallas_call(
        pack_kernel,
        out_shape=(
            jax.ShapeDtypeStruct((16, SENT, C), BF),
            jax.ShapeDtypeStruct((2, PAD, C), BF),
        ),
        in_specs=[pl.BlockSpec(memory_space=pltpu.SMEM)] + [vmem] * 6,
        out_specs=(vmem, vmem),
    )(place, so2_zero, so2_one, so2_two, feat_in, ffn_in, grad_out)


def join_kernel(place, own_ref, other_ref, whole_ref, half_ref, feat_ref):
    core = place[0]
    share = place[2]

    def fill(side, ref, this_share):
        def pair(z_row, first, rows):
            return jnp.concatenate(
                [
                    ref[2 * z_row, first : first + rows, :],
                    ref[2 * z_row + 1, first : first + rows, :],
                ],
                axis=0,
            )

        def put(z_row, start, first, rows):
            block = pair(z_row, first, rows)
            at = start + 2 * rows * z_row
            whole_ref[side, at : at + 2 * rows, :] = block
            at = start // 2 + 2 * rows * (z_row % 4)

            @pl.when(core == z_row // 4)
            def _():
                half_ref[side, at : at + 2 * rows, :] = block

        for z_row in range(8):
            put(z_row, 0, 0, 56)
            put(z_row, AT_ONE, 56, 48)
            put(z_row, AT_TWO, 104, 40)

        @pl.when(this_share < 4)
        def _():
            for z_row in range(8):
                put(z_row, AT_MORE, 144, 48)

        @pl.when((this_share >= 4) & (this_share < 6))
        def _():
            for z_row in range(8):
                put(z_row, AT_MORE, 144, 40)

        @pl.when((this_share >= 6))
        def _():
            whole_ref[side, AT_MORE:WHOLE, :] = jnp.zeros((WHOLE - AT_MORE, C), BF)
            half_ref[side, AT_MORE // 2 : WHOLE // 2, :] = jnp.zeros(((WHOLE - AT_MORE) // 2, C), BF)

        @pl.when((this_share >= 4) & (this_share < 6))
        def _():
            whole_ref[side, AT_MORE + 640 : WHOLE, :] = jnp.zeros((128, C), BF)
            half_ref[side, AT_MORE // 2 + 320 : WHOLE // 2, :] = jnp.zeros((64, C), BF)

    fill(0, own_ref, share)
    fill(1, other_ref, share + 1 - 2 * core)
    for peer in range(16):
        feat_ref[peer] = own_ref[peer, SHARE:SENT, :]


def join_shares(place, own, other):
    vmem = pl.BlockSpec(memory_space=VMEM)
    return pl.pallas_call(
        join_kernel,
        out_shape=(
            jax.ShapeDtypeStruct((2, WHOLE, C), BF),
            jax.ShapeDtypeStruct((2, WHOLE // 2, C), BF),
            jax.ShapeDtypeStruct((16, PAD, C), BF),
        ),
        in_specs=[pl.BlockSpec(memory_space=pltpu.SMEM), vmem, vmem],
        out_specs=(vmem,) * 3,
        compiler_params=grant(16),
    )(place, own, other)


def ffn_kernel(own_ref, other_ref, up_ref, down_ref, to_ref, from_ref, back_ref, out_ref):
    for place, ref in ((0, own_ref), (1, other_ref)):
        grid_feat = dot(to_ref[...], ref[0]).astype(BF)
        grad_value = dot(from_ref[...], ref[1]).astype(BF)
        pre_act = dot(grid_feat, up_ref[...])
        grad_act = dot_nt(grad_value, down_ref[...])
        gate = jax.nn.sigmoid(pre_act)
        grad_pre = (grad_act * gate * (1.0 + pre_act * (1.0 - gate))).astype(BF)
        grad_grid = dot_nt(grad_pre, up_ref[...]).astype(BF)
        out_ref[place] = (ref[1].astype(F32) + dot(back_ref[...], grad_grid)).astype(BF)


def ffn_backward(own, other, ffn_up, ffn_down):
    to_grid, from_grid = sphere_tables(LMAX, GRID_SIDE)
    points = to_grid.shape[0]
    to_pad = np.zeros((208, PAD), np.float32)
    to_pad[:points, :COEF] = to_grid
    from_pad = np.zeros((208, PAD), np.float32)
    from_pad[:points, :COEF] = from_grid.T
    back_pad = np.ascontiguousarray(to_pad.T)
    tables = [jnp.asarray(table, F32).astype(BF) for table in (to_pad, from_pad, back_pad)]
    return pl.pallas_call(
        ffn_kernel,
        out_shape=jax.ShapeDtypeStruct((2, PAD, C), BF),
        in_specs=[pl.BlockSpec(memory_space=VMEM)] * 7,
        out_specs=pl.BlockSpec(memory_space=VMEM),
        compiler_params=grant(16),
    )(own, other, ffn_up, ffn_down, *tables)


def rotate_kernel(
    src, tgt, ang, feat_ref, y0_ref, y1_ref, y2_ref, y3_ref, wig_ref, rot_ref, go_ref, acc, grad_ref
):
    slots = 128
    for back, ref in enumerate((y0_ref, y1_ref, y2_ref, y3_ref)):
        grad_ref[8 * back : 8 * back + 8] = ref[...]

    def body(step, carry):
        for lane in range(8):
            slot = step * 8 + lane
            rows = jnp.concatenate([feat_ref[src[slot]], grad_ref[tgt[slot]]], axis=1)
            turned = dot(wig_ref[ang[slot]], rows)
            acc[pl.ds(slot, 32, stride=slots), :] = turned[:, :C]
            go_ref[pl.ds(slot, 32, stride=slots), :] = turned[:, C:]
        return carry

    lax.fori_loop(0, slots // 8, body, 0)
    rot_ref[...] = acc[...].astype(BF)


def rotate_slots(src, tgt, ang, feat, grads, wig):
    smem = pl.BlockSpec(memory_space=pltpu.SMEM)
    vmem = pl.BlockSpec(memory_space=VMEM)
    return pl.pallas_call(
        rotate_kernel,
        out_shape=(
            jax.ShapeDtypeStruct((32 * 128, C), BF),
            jax.ShapeDtypeStruct((32 * 128, C), F32),
        ),
        in_specs=[smem] * 3 + [vmem] * 6,
        out_specs=(vmem, vmem),
        scratch_shapes=[VMEM((32 * 128, C), F32), VMEM((32, PAD, C), BF)],
        compiler_params=grant(16),
    )(src, tgt, ang, feat, *grads, wig)


def edge_kernel(
    place, src, ang, own_ref, near_ref, far_ref, half_ref, half_far_ref,
    rot_ref, go_ref, radial_ref, wig_ref, out_ref,
    w_zero, w_one, w_two, hidden, grad_rot, acc,
):
    core = place[0]
    quarter = place[1]

    def take(ref, at, ahead, side, half):
        share = 2 * lax.rem(quarter + ahead, 4) + side
        cut = 1 if half is None else 2

        def move(weight, block, first, rows):
            rows = rows // cut
            start = 0 if half is None else pl.multiple_of(rows * half, 64)
            weight[block, pl.ds(start, rows), :] = ref[at, first // cut : first // cut + rows, :]

        move(w_zero, share, 0, 896)
        move(w_one, share, AT_ONE, 768)
        move(w_two, share, AT_TWO, 640)

        @pl.when(share < 4)
        def _():
            move(w_one, 8 + share, AT_MORE, 768)

        @pl.when((share >= 4) & (share < 6))
        def _():
            move(w_two, 4 + share, AT_MORE, 640)

    for at in range(2):
        side = core if at == 0 else 1 - core
        take(own_ref, at, 0, side, None)
        take(near_ref, at, 3 - 2 * core, side, None)
        take(far_ref, at, 1 + 2 * core, 1 - side, None)
        take(half_ref, at, 2, side, core)
        take(half_far_ref, at, 2, 1 - side, 1 - core)

    def columns(weight, first, count, rows):
        return jnp.concatenate([weight[first + at, rows, :] for at in range(count)], axis=1)

    every = slice(None)

    def turned(first, count):
        return jnp.concatenate(
            [rot_ref[128 * row : 128 * row + 128, :] for row in range(first, first + count)], axis=1
        )

    radial = radial_ref[...].astype(F32)

    def put(first, rows, value):
        for row in range(rows):
            hidden[128 * (first + row) : 128 * (first + row) + 128, :] = (
                value[:, 128 * row : 128 * row + 128] * radial
            )

    left = turned(0, 7)
    for pair in range(4):
        put(2 * pair, 2, dot(left, columns(w_zero, 2 * pair, 2, every)))

    def higher(first, count, weight, hidden_first):
        plus = turned(first, count)
        minus = turned(first + count, count)
        both = jnp.concatenate(
            [jnp.concatenate([plus, -minus], axis=1), jnp.concatenate([minus, plus], axis=1)], axis=0
        )
        start = 0
        while start < count:
            wide = min(2, count - start)
            value = dot(
                both,
                jnp.concatenate(
                    [columns(weight, start, wide, every), columns(weight, count + start, wide, every)],
                    axis=0,
                ),
            )
            put(hidden_first + start, wide, value[:128])
            put(hidden_first + count + start, wide, value[128:])
            start = start + wide

    higher(7, 6, w_one, 8)
    higher(19, 5, w_two, 20)

    def hid(row):
        return hidden[128 * row : 128 * row + 128, :]

    def go(row):
        return go_ref[128 * row : 128 * row + 128, :] * message_scale

    scalar_pre = hid(0)
    sigmoid_scalar = jax.nn.sigmoid(scalar_pre)
    sigmoid_gate = jax.nn.sigmoid(hid(7))
    weight_gate = sigmoid_gate * radial
    grads = {}
    grads[0] = (
        go(0) * sigmoid_scalar * (1.0 + scalar_pre * (1.0 - sigmoid_scalar)) * radial
    ).astype(BF)
    total = jnp.zeros((128, C), F32)
    for kept in range(1, KEEP):
        row = kept if kept < 7 else kept + 1
        value = go(kept)
        total = total + value * hid(row)
        grads[row] = (value * weight_gate).astype(BF)
    grads[7] = (total * sigmoid_gate * (1.0 - sigmoid_gate) * radial).astype(BF)

    def side_by_side(first, count):
        return jnp.concatenate([grads[row] for row in range(first, first + count)], axis=1)

    def keep(first, value):
        for row in range(value.shape[1] // 128):
            grad_rot[128 * (first + row) : 128 * (first + row) + 128, :] = value[
                :, 128 * row : 128 * row + 128
            ]

    right = side_by_side(0, 8)
    for start in (0, 2, 4, 6):
        wide = min(2, 7 - start)
        rows = slice(128 * start, 128 * (start + wide))
        keep(start, dot_nt(right, columns(w_zero, 0, 8, rows)))

    def back(first, count, weight, hidden_first):
        both = jnp.concatenate(
            [side_by_side(hidden_first, count), side_by_side(hidden_first + count, count)], axis=0
        )
        start = 0
        while start < count:
            wide = min(2, count - start)
            rows = slice(128 * start, 128 * (start + wide))
            real = dot_nt(both, columns(weight, 0, count, rows))
            imag = dot_nt(both, columns(weight, count, count, rows))
            keep(first + start, real[:128] + imag[128:])
            keep(first + count + start, real[128:] - imag[:128])
            start = start + wide

    back(7, 6, w_one, 8)
    back(19, 5, w_two, 20)
    grad_rot[KEEP * 128 :, :] = jnp.zeros((3 * 128, C), F32)

    acc[...] = jnp.zeros_like(acc)
    live = place[3]

    def slot_body(step, carry):
        for lane in range(8):
            slot = step * 8 + lane
            rows = grad_rot[pl.ds(slot, 32, stride=128), :]
            rows = jnp.where(slot < live, rows, 0.0).astype(BF)
            acc[src[slot]] += dot(wig_ref[ang[slot]], rows)
        return carry

    lax.fori_loop(0, lax.div(live + 7, 8), slot_body, 0)
    out_ref[...] = acc[...].astype(BF)


def edge_backward(place, src, ang, shares, rot, go, radial, wig_back):
    smem = pl.BlockSpec(memory_space=pltpu.SMEM)
    vmem = pl.BlockSpec(memory_space=VMEM)
    return pl.pallas_call(
        edge_kernel,
        out_shape=jax.ShapeDtypeStruct((16, PAD, C), BF),
        in_specs=[smem] * 3 + [vmem] * 9,
        out_specs=vmem,
        scratch_shapes=[
            VMEM((8, 896, C), BF),
            VMEM((12, 768, C), BF),
            VMEM((10, 640, C), BF),
            VMEM((30 * 128, C), F32),
            VMEM((32 * 128, C), F32),
            VMEM((16, PAD, C), F32),
        ],
        compiler_params=grant(28),
    )(place, src, ang, *shares, rot, go, radial, wig_back)


def shift(value, axis, count, step):
    return lax.ppermute(value, axis, [(at, (at + step) % count) for at in range(count)])


def swap(value, axis):
    return lax.ppermute(value, axis, [(0, 1), (1, 0)])


def body(
    feat_in, ffn_in, grad_out, ffn_up, ffn_down, so2_zero, so2_one, so2_two, wigner,
    edge_src, edge_tgt, edge_angle, edge_radial, edge_count,
):
    core = lax.axis_index("core").astype(jnp.int32)
    x_here = lax.axis_index("x").astype(jnp.int32)
    y_hi = lax.axis_index("yhi").astype(jnp.int32)
    quarter = (x_here + 2 * y_hi) % 4
    place = jnp.stack([core, quarter, 2 * quarter + core, edge_count.reshape(())])

    sent, pair = pack_own(place, so2_zero, so2_one, so2_two, feat_in, ffn_in, grad_out)
    pair_other = swap(pair, "core")
    got = lax.all_to_all(sent, ("z", "ylo"), 0, 0, tiled=True)
    target_grads = ffn_backward(pair, pair_other, ffn_up, ffn_down)
    grads = target_grads
    for axis in ("x", "yhi"):
        blocks = [grads]
        for step in (1, 2, 3):
            blocks.append(shift(grads, axis, 4, step))
        if axis == "x":
            grads = jnp.concatenate(blocks, axis=0)
    got_other = swap(got, "core")
    own, half, feat = join_shares(place, got, got_other)
    turn = [(2 * at, 2 * ((at + 1) % 4)) for at in range(4)]
    turn = turn + [(2 * at + 1, 2 * ((at + 3) % 4) + 1) for at in range(4)]
    near = lax.ppermute(own, ("x", "core"), turn)
    half_near = lax.ppermute(half, ("yhi", "core"), turn)
    far = swap(near, "core")
    half_far = swap(half_near, "core")
    shares = (own, near, far, half_near, half_far)

    src_slots = edge_src.reshape(-1)
    tgt_slots = edge_tgt.reshape(-1)
    angle_slots = edge_angle.reshape(-1)
    y_back = (y_hi - tgt_slots // 8) % 4
    x_back = (x_here - tgt_slots // 2 % 4) % 4
    tgt_piece = (y_back * 4 + x_back) * 2 + ((tgt_slots % 2) ^ core)
    wig = jnp.pad(wigner, ((0, 0), (0, 32 - KEEP), (0, PAD - COEF)))
    wig_back = jnp.transpose(wig, (0, 2, 1))
    rot, go = rotate_slots(src_slots, tgt_piece, angle_slots, feat, blocks, wig)
    partial_sum = edge_backward(
        place, src_slots, angle_slots, shares, rot, go, edge_radial.reshape(128, C), wig_back
    )
    parts = lax.all_to_all(partial_sum, ("z", "ylo"), 0, 0, tiled=True)
    total = target_grads[0].astype(F32) + jnp.sum(parts.astype(F32), axis=0)
    return total[None, :COEF].astype(BF)


def solution(mesh):
    devices = mesh.devices.reshape(4, 4, 2, 8, 2)
    fine = Mesh(devices, ("yhi", "x", "core", "z", "ylo"))
    src = ("yhi", "x", "core")
    tgt = ("z", "ylo")
    placed = (
        P(src + tgt, None, None),
        P(src + tgt, None, None),
        P(src + tgt, None, None),
        P(),
        P(),
        P(tgt, None),
        P(None, tgt, None),
        P(None, tgt, None),
        P(),
        P(src, tgt, None),
        P(src, tgt, None),
        P(src, tgt, None),
        P(src, tgt, None, None),
        P(src, tgt),
    )
    return jax.shard_map(
        body,
        mesh=fine,
        in_specs=placed,
        out_specs=P(src + tgt, None, None),
        check_vma=False,
    )
```
